32 devices in a mesh: row: 2 (over y), col: 16 (over z, x, core).
Axes of the slice: x: 2, y: 2, z: 4, core: 2. Of those that a mesh axis runs over, the one named last changes fastest.
Arguments:
- object_field: float32 [2, 512, 4096], P(None, 'row', 'col'), may hold values from -6 to 6
- probe_field: float32 [2, 256, 256], replicated, may hold values from -4.2 to 4.2
- amplitudes: bfloat16 [2, 16, 6, 256, 256], P('row', 'col'), may hold values from 0 to 2
- offsets: int32 [2, 16, 6, 2], P('row', 'col'), may hold values from 0 to 256
- counts: int32 [2, 16], P('row', 'col'), may hold values from 2 to 6
Outputs:
- updated_object: float32 [2, 512, 4096], P(None, 'row', 'col')
The draws below stay inside these ranges and needn't reach their ends.
Inputs may be any that keep to these rules, and one draw needn't show every extreme that they name: offsets[r, c, k] places slot k of tile (r, c) as stated in the reference program, so a patch reaches at most 128 pixels beyond its tile. Tile (r, c) uses slots 0 to counts[r, c] - 1; offsets and amplitudes of the other slots are ignored.
All inputs are finite; a program needn't handle non-finite values.
Results may differ from the reference program's by a relative error of at most 0.0021.
Values sent between devices are 32-bit elements; how exact they have to be, the bound alone decides.
A program may use at most 64 MiB of HBM per device.

```python
import math
import jax
import jax.numpy as jnp
from jax import lax

TILE = 256
RIM = 128
MAXPOS = 6
ITERS = 2
TILES_R = 2
TILES_C = 16


def place_ends(entries, key, low, top_value):
    longest = entries.shape.index(max(entries.shape))
    spots = []
    for shift in (0, 1):
        where = [jax.random.randint(jax.random.fold_in(key, axis), (), 0, length) for axis, length in enumerate(entries.shape)]
        where[longest] = (where[longest] + shift) % entries.shape[longest]
        spots.append(tuple(where))
    return entries.at[spots[0]].set(low).at[spots[1]].set(top_value)


def steps_of(key, dims, split, least, high):
    loudness = 1.0
    for axis_at, parts in split:
        steps = jax.random.uniform(jax.random.fold_in(jax.random.fold_in(key, 6), axis_at), (parts,), jnp.float32, least / len(split), high / len(split))
        loudness = loudness * jnp.repeat(jnp.exp(steps), dims[axis_at] // parts).reshape((-1,) + (1,) * (len(dims) - 1 - axis_at))
    return loudness


def bell_draw(own_key, extent, scale, limit, cuts=(), kind=jnp.bfloat16):
    factor_of = steps_of(own_key, extent, cuts, -0.22, 0.18) if cuts else 1.0
    drawn = jax.random.normal(own_key, extent, jnp.float32) * scale * factor_of
    return jnp.minimum(jnp.maximum(drawn, -limit), limit).astype(kind)


def setup_inputs(seed: int = 0) -> dict:
    arg_keys = jax.random.split(jax.random.key(seed), 6)
    return {
        "object_field": bell_draw(arg_keys[0], (2, TILES_R * TILE, TILES_C * TILE), 1.0, 6.0, ((1, 2), (2, 16)), jnp.float32),
        "probe_field": bell_draw(arg_keys[1], (2, TILE, TILE), 0.7, 4.2, (), jnp.float32),
        "amplitudes": jnp.clip(2.0 * jax.random.uniform(arg_keys[2], (TILES_R, TILES_C, MAXPOS, TILE, TILE), jnp.float32) ** steps_of(arg_keys[2], (TILES_R, TILES_C, MAXPOS, TILE, TILE), ((0, 2), (1, 16)), -0.2, 0.2), 0.0, 2.0).astype(jnp.bfloat16),
        "offsets": place_ends(jax.random.randint(arg_keys[3], (TILES_R, TILES_C, MAXPOS, 2), 0, TILE + 1), jax.random.fold_in(arg_keys[3], 1), 0, TILE).astype(jnp.int32),
        "counts": place_ends(jax.random.randint(arg_keys[4], (TILES_R, TILES_C), 2, MAXPOS + 1), jax.random.fold_in(arg_keys[4], 1), 2, MAXPOS).astype(jnp.int32),
    }


smooth_term = 0.25
step_size = 0.5
regular_term = 1.0

def dft_table(length):
    positions = jnp.arange(length, dtype=jnp.int32)
    phase_step = positions[:, None] * positions[None, :] % length
    phase_angle = phase_step.astype(jnp.float32) * (2.0 * math.pi / length)
    norm_scale = 1.0 / math.sqrt(length)
    cosine = jnp.cos(phase_angle) * norm_scale
    sine_part = jnp.sin(phase_angle) * norm_scale
    return jnp.stack([jnp.stack([cosine, sine_part]), jnp.stack([-sine_part, cosine])]).astype(jnp.bfloat16)

def transform(field, matrices, inverse):
    if inverse:
        first_form = 'pqab,spbc->sqac'
        second_form = 'spab,pqbc->sqac'
    else:
        first_form = 'qpab,spbc->sqac'
        second_form = 'spab,qpbc->sqac'
    wide_table = matrices.astype(jnp.float32)
    half_done = jnp.einsum(first_form, wide_table, field.astype(jnp.float32), precision=lax.Precision.HIGHEST).astype(jnp.bfloat16)
    return jnp.einsum(second_form, half_done.astype(jnp.float32), wide_table, precision=lax.Precision.HIGHEST)

def patch_gradients(patches, probe_field, amplitudes, in_use, matrices):
    probe_real = probe_field[0]
    probe_imag = probe_field[1]
    object_real = patches[:, 0]
    object_imag = patches[:, 1]
    exit_wave = jnp.stack([probe_real * object_real - probe_imag * object_imag, probe_real * object_imag + probe_imag * object_real], axis=1).astype(jnp.bfloat16)
    spectrum = transform(exit_wave, matrices, False)
    modulus = jnp.sqrt(spectrum[:, 0] * spectrum[:, 0] + spectrum[:, 1] * spectrum[:, 1] + smooth_term)
    factor = (1.0 - amplitudes.astype(jnp.float32) / modulus) * in_use[:, None, None]
    residual = (spectrum * factor[:, None]).astype(jnp.bfloat16)
    back_wave = transform(residual, matrices, True)
    return jnp.stack([probe_real * back_wave[:, 0] + probe_imag * back_wave[:, 1], probe_real * back_wave[:, 1] - probe_imag * back_wave[:, 0]], axis=1)

def reference(object_field, probe_field, amplitudes, offsets, counts):
    matrices = dft_table(TILE)
    tile_total = TILES_R * TILES_C
    flat_offsets = offsets.reshape(tile_total, MAXPOS, 2)
    flat_counts = counts.reshape(tile_total)
    flat_amps = amplitudes.reshape(tile_total, MAXPOS, TILE, TILE)
    slot_index = jnp.arange(MAXPOS, dtype=jnp.int32)
    probe_power = probe_field[0] * probe_field[0] + probe_field[1] * probe_field[1]
    padded_rows = TILES_R * TILE + 2 * RIM
    padded_cols = TILES_C * TILE + 2 * RIM
    zero_index = jnp.zeros((), jnp.int32)
    tile_ids = jnp.arange(tile_total, dtype=jnp.int32)

    def corners(tile_id):
        tile_row = tile_id // TILES_C
        tile_col = tile_id % TILES_C
        top_rows = (tile_row * TILE + flat_offsets[tile_id, :, 0]).astype(jnp.int32)
        left_cols = (tile_col * TILE + flat_offsets[tile_id, :, 1]).astype(jnp.int32)
        in_use = (slot_index < flat_counts[tile_id]).astype(jnp.float32)
        return (top_rows, left_cols, in_use)

    def light_step(grid, tile_id):
        top_rows, left_cols, in_use = corners(tile_id)

        def add_light(slot, inner):
            window = lax.dynamic_slice(inner, (top_rows[slot], left_cols[slot]), (TILE, TILE))
            return lax.dynamic_update_slice(inner, window + probe_power * in_use[slot], (top_rows[slot], left_cols[slot]))
        return (lax.fori_loop(0, MAXPOS, add_light, grid), None)
    light_grid, leftover = lax.scan(light_step, jnp.zeros((padded_rows, padded_cols), jnp.float32), tile_ids)
    illumination = light_grid[RIM:RIM + TILES_R * TILE, RIM:RIM + TILES_C * TILE]
    for iteration in range(ITERS):
        padded_object = jnp.pad(object_field, ((0, 0), (RIM, RIM), (RIM, RIM)))

        def grad_step(grid, tile_id):
            top_rows, left_cols, in_use = corners(tile_id)

            def cut_patch(top_row, left_col):
                return lax.dynamic_slice(padded_object, (zero_index, top_row, left_col), (2, TILE, TILE))
            patches = jax.vmap(cut_patch)(top_rows, left_cols)
            pieces = patch_gradients(patches, probe_field, flat_amps[tile_id], in_use, matrices)

            def add_piece(slot, inner):
                where_to = (zero_index, top_rows[slot], left_cols[slot])
                window = lax.dynamic_slice(inner, where_to, (2, TILE, TILE))
                return lax.dynamic_update_slice(inner, window + pieces[slot], where_to)
            return (lax.fori_loop(0, MAXPOS, add_piece, grid), None)
        grad_grid, leftover = lax.scan(grad_step, jnp.zeros((2, padded_rows, padded_cols), jnp.float32), tile_ids)
        gradient = grad_grid[:, RIM:RIM + TILES_R * TILE, RIM:RIM + TILES_C * TILE]
        object_field = object_field - step_size * gradient / (illumination + regular_term)
    return object_field
```

```python
import functools
import math

import jax
import jax.numpy as jnp
import numpy as np
from jax import lax
from jax.experimental import pallas as pl
from jax.experimental.pallas import tpu as pltpu
from jax.sharding import PartitionSpec as P

TILE = 256
RIM = 128
MAXPOS = 6
ITERS = 2
LANES = 128
CHUNK = 64

smooth_term = 0.25
step_size = 0.5
regular_term = 1.0

AXES = ("row", "col")
SIDES = [(-1, 0), (1, 0), (0, -1), (0, 1), (-1, -1), (-1, 1), (1, -1), (1, 1)]


def dft_tables():
    positions = np.arange(TILE)
    phase_step = (positions[:, None] * positions[None, :]) % TILE
    angle = phase_step.astype(np.float32) * np.float32(2.0 * math.pi / TILE)
    scale = np.float32(1.0 / math.sqrt(TILE))
    real = np.cos(angle).astype(np.float32) * scale
    imag = -np.sin(angle).astype(np.float32) * scale
    return np.stack([real, imag]).astype(jnp.bfloat16)


def edge(step, length):
    if step < 0:
        return slice(0, RIM)
    if step > 0:
        return slice(length - RIM, length)
    return slice(0, length)


def zone(step):
    return (slice(0, RIM), slice(RIM, RIM + TILE), slice(RIM + TILE, 2 * RIM + TILE))[step + 1]


def shape_of(planes, side):
    return (planes, TILE if side[0] == 0 else RIM, TILE if side[1] == 0 else RIM)


def exchange(pieces):
    rows, cols = lax.axis_size("row"), lax.axis_size("col")
    out = []
    for piece, (down, right) in zip(pieces, SIDES):
        pairs = [
            (r * cols + c, (r + down) * cols + c + right)
            for r in range(rows)
            for c in range(cols)
            if 0 <= r + down < rows and 0 <= c + right < cols
        ]
        out.append(lax.ppermute(piece, AXES, pairs))
    return out


def cut_edges(field_ref, out_refs):
    for side, out in zip(SIDES, out_refs):
        out[...] = field_ref[:, edge(side[0], TILE), edge(side[1], TILE)]


def edges_kernel(field_ref, *out_refs):
    cut_edges(field_ref, out_refs)


def gradient_kernel(
    planes, offs, cnt, own, *refs
):
    halos = refs[:8]
    probe, amps, table = refs[8:11]
    center_out = refs[11]
    outs = refs[12:20]
    ext, canvas, left_m, right_m, wave, half, full = refs[20:]

    real, imag = table[0], table[1]
    left_m[:TILE, :TILE] = real
    left_m[:TILE, TILE:] = -imag
    left_m[TILE:, :TILE] = imag
    left_m[TILE:, TILE:] = real
    right_m[:TILE, :TILE] = real
    right_m[:TILE, TILE:] = imag
    right_m[TILE:, :TILE] = -imag
    right_m[TILE:, TILE:] = real

    canvas[...] = jnp.zeros_like(canvas)
    ext[:, 4] = jnp.zeros_like(ext[:, 4])
    for block in range(2):
        ext[:, 1 + block, RIM : RIM + TILE, :] = own[:, :, block * LANES : (block + 1) * LANES]
    for (down, right), halo in zip(SIDES, halos):
        rows = zone(-down)
        if right == 0:
            ext[:, 1, rows, :] = halo[:, :, :LANES]
            ext[:, 2, rows, :] = halo[:, :, LANES:]
        else:
            ext[:, 3 if right < 0 else 0, rows, :] = halo[...]

    lane = lax.broadcasted_iota(jnp.int32, (CHUNK, LANES), 1)

    def one_slot(slot, carry):
        top = offs[slot, 0]
        left = offs[slot, 1]
        first = left // LANES
        shift = left % LANES
        back = (LANES - shift) % LANES
        keep = lane < LANES - shift
        late = lane >= shift
        for at in range(0, TILE, CHUNK):
            rows = pl.ds(top + at, CHUNK)
            parts = []
            for p in range(2):
                rolled = [
                    pltpu.roll(ext[p, first + b, rows, :], back, 1) for b in range(3)
                ]
                parts.append([jnp.where(keep, rolled[b], rolled[b + 1]) for b in range(2)])
            for b in range(2):
                cols = slice(b * LANES, (b + 1) * LANES)
                pr = probe[0, at : at + CHUNK, cols]
                pi = probe[1, at : at + CHUNK, cols]
                wr, wi = parts[0][b], parts[1][b]
                wave[at : at + CHUNK, cols] = (pr * wr - pi * wi).astype(jnp.bfloat16)
                wave[TILE + at : TILE + at + CHUNK, cols] = (pr * wi + pi * wr).astype(jnp.bfloat16)

        def by_rows(matrix):
            product = jnp.dot(matrix[...], wave[...], preferred_element_type=jnp.float32)
            half[:, :TILE] = product[:TILE].astype(jnp.bfloat16)
            half[:, TILE:] = product[TILE:].astype(jnp.bfloat16)

        def by_cols(matrix):
            full[...] = jnp.dot(half[...], matrix[...], preferred_element_type=jnp.float32)

        by_rows(left_m)
        by_cols(right_m)
        for at in range(0, TILE, CHUNK):
            sr = full[at : at + CHUNK, :TILE]
            si = full[at : at + CHUNK, TILE:]
            amp = amps[slot, at : at + CHUNK, :].astype(jnp.float32)
            factor = 1.0 - amp * lax.rsqrt(sr * sr + si * si + smooth_term)
            wave[at : at + CHUNK, :] = (sr * factor).astype(jnp.bfloat16)
            wave[TILE + at : TILE + at + CHUNK, :] = (si * factor).astype(jnp.bfloat16)
        by_rows(right_m)
        by_cols(left_m)
        for at in range(0, TILE, CHUNK):
            rows = pl.ds(top + at, CHUNK)
            pieces = [[] for _ in range(planes)]
            for b in range(2):
                cols = slice(b * LANES, (b + 1) * LANES)
                pr = probe[0, at : at + CHUNK, cols]
                pi = probe[1, at : at + CHUNK, cols]
                br = full[at : at + CHUNK, cols]
                bi = full[at : at + CHUNK, TILE + b * LANES : TILE + (b + 1) * LANES]
                pieces[0].append(pltpu.roll(pr * br + pi * bi, shift, 1))
                pieces[1].append(pltpu.roll(pr * bi - pi * br, shift, 1))
                if planes > 2:
                    pieces[2].append(pltpu.roll(pr * pr + pi * pi, shift, 1))
            for p in range(planes):
                a, b = pieces[p]
                canvas[p, first, rows, :] += jnp.where(late, a, 0.0)
                canvas[p, first + 1, rows, :] += jnp.where(late, b, a)
                canvas[p, first + 2, rows, :] += jnp.where(late, 0.0, b)
        return carry

    lax.fori_loop(0, cnt[0], one_slot, 0)

    center_out[:, :, :LANES] = canvas[:, 1, RIM : RIM + TILE, :]
    center_out[:, :, LANES:] = canvas[:, 2, RIM : RIM + TILE, :]
    for (down, right), out in zip(SIDES, outs):
        rows = zone(down)
        if right == 0:
            out[:, :, :LANES] = canvas[:, 1, rows, :]
            out[:, :, LANES:] = canvas[:, 2, rows, :]
        else:
            out[...] = canvas[:, 0 if right < 0 else 3, rows, :]


def update_kernel(first, last, own, center, *refs):
    pieces = refs[:8]
    refs = refs[8:]
    if not first:
        scale_in = refs[0]
        refs = refs[1:]
    new = refs[0]
    refs = refs[1:]
    total = refs[-1]
    total[...] = center[...]
    for (down, right), piece in zip(SIDES, pieces):
        total[:, edge(-down, TILE), edge(-right, TILE)] += piece[...]
    if first:
        scale = step_size / (total[2] + regular_term)
        refs[0][...] = scale
        refs = refs[1:]
    else:
        scale = scale_in[...]
    for p in range(2):
        new[p] = own[p] - total[p] * scale
    if not last:
        cut_edges(new, refs[:8])


def vmem(count):
    return [pl.BlockSpec(memory_space=pltpu.VMEM)] * count


def f32(shape):
    return jax.ShapeDtypeStruct(shape, jnp.float32)


def per_device(object_field, probe_field, amplitudes, offsets, counts):
    table = jnp.asarray(dft_tables())
    offs = offsets.reshape(MAXPOS, 2)
    cnt = counts.reshape(1)
    amps = amplitudes.reshape(MAXPOS, TILE, TILE)
    field = object_field
    edge_shapes = [f32(shape_of(2, side)) for side in SIDES]
    edges = pl.pallas_call(
        edges_kernel, out_shape=edge_shapes, in_specs=vmem(1), out_specs=vmem(8), name="edges"
    )(field)
    scale = None
    for iteration in range(ITERS):
        first, last = iteration == 0, iteration == ITERS - 1
        planes = 3 if first else 2
        halos = exchange(edges)
        center, *pieces = pl.pallas_call(
            functools.partial(gradient_kernel, planes),
            out_shape=[f32((planes, TILE, TILE))] + [f32(shape_of(planes, s)) for s in SIDES],
            in_specs=[pl.BlockSpec(memory_space=pltpu.SMEM)] * 2 + vmem(12),
            out_specs=vmem(9),
            scratch_shapes=[
                pltpu.VMEM((2, 5, 2 * TILE, LANES), jnp.float32),
                pltpu.VMEM((planes, 5, 2 * TILE, LANES), jnp.float32),
                pltpu.VMEM((2 * TILE, 2 * TILE), jnp.bfloat16),
                pltpu.VMEM((2 * TILE, 2 * TILE), jnp.bfloat16),
                pltpu.VMEM((2 * TILE, TILE), jnp.bfloat16),
                pltpu.VMEM((TILE, 2 * TILE), jnp.bfloat16),
                pltpu.VMEM((TILE, 2 * TILE), jnp.float32),
            ],
            name=f"gradient{iteration}",
        )(offs, cnt, field, *halos, probe_field, amps, table)
        pieces = exchange(pieces)
        operands = [field, center, *pieces] + ([] if first else [scale])
        shapes = [f32((2, TILE, TILE))]
        if first:
            shapes.append(f32((TILE, TILE)))
        if not last:
            shapes += edge_shapes
        results = pl.pallas_call(
            functools.partial(update_kernel, first, last),
            out_shape=shapes,
            in_specs=vmem(len(operands)),
            out_specs=vmem(len(shapes)),
            scratch_shapes=[pltpu.VMEM((planes, TILE, TILE), jnp.float32)],
            name=f"update{iteration}",
        )(*operands)
        field = results[0]
        rest = results[1:]
        if first:
            scale, rest = rest[0], rest[1:]
        edges = rest
    return field


def solution(mesh):
    in_specs = (
        P(None, "row", "col"),
        P(),
        P("row", "col", None, None, None),
        P("row", "col", None, None),
        P("row", "col"),
    )
    out_specs = P(None, "row", "col")
    return jax.shard_map(
        per_device, mesh=mesh, in_specs=in_specs, out_specs=out_specs, check_vma=False
    )
```

```python
import functools
import math

import jax
import jax.numpy as jnp
import numpy as np
from jax import lax
from jax.experimental import pallas as pl
from jax.experimental.pallas import tpu as pltpu
from jax.sharding import PartitionSpec as P

TILE = 256
RIM = 128
MAXPOS = 6
ITERS = 2
LANES = 128
CHUNK = 64

smooth_term = 0.25
step_size = 0.5
regular_term = 1.0

AXES = ("row", "col")
SIDES = [(-1, 0), (1, 0), (0, -1), (0, 1), (-1, -1), (-1, 1), (1, -1), (1, 1)]


def dft_tables():
    positions = np.arange(TILE)
    phase_step = (positions[:, None] * positions[None, :]) % TILE
    angle = phase_step.astype(np.float32) * np.float32(2.0 * math.pi / TILE)
    scale = np.float32(1.0 / math.sqrt(TILE))
    real = np.cos(angle).astype(np.float32) * scale
    imag = -np.sin(angle).astype(np.float32) * scale
    return np.stack([real, imag]).astype(jnp.bfloat16)


def edge(step, length):
    if step < 0:
        return slice(0, RIM)
    if step > 0:
        return slice(length - RIM, length)
    return slice(0, length)


def zone(step):
    return (slice(0, RIM), slice(RIM, RIM + TILE), slice(RIM + TILE, 2 * RIM + TILE))[step + 1]


def shape_of(planes, side):
    return (planes, TILE if side[0] == 0 else RIM, TILE if side[1] == 0 else RIM)


def inside(row, col):
    rows, cols = lax.axis_size("row"), lax.axis_size("col")
    return (row >= 0) & (row < rows) & (col >= 0) & (col < cols)


def exchange(sources, landings, sends, receives):
    row, col = lax.axis_index("row"), lax.axis_index("col")
    barrier = pltpu.get_barrier_semaphore()
    for down, right in SIDES:

        @pl.when(inside(row + down, col + right))
        def _():
            pl.semaphore_signal(
                barrier,
                inc=1,
                device_id=(row + down, col + right),
                device_id_type=pl.DeviceIdType.MESH,
            )

    peers = 0
    for down, right in SIDES:
        peers = peers + jnp.where(inside(row + down, col + right), 1, 0)
    pl.semaphore_wait(barrier, peers)

    def copy_of(i, down, right):
        return pltpu.make_async_remote_copy(
            src_ref=sources[i],
            dst_ref=landings[i],
            send_sem=sends.at[i],
            recv_sem=receives.at[i],
            device_id=(row + down, col + right),
            device_id_type=pl.DeviceIdType.MESH,
        )

    for i in (4, 5, 6, 7, 0, 1, 2, 3):
        down, right = SIDES[i]

        @pl.when(inside(row + down, col + right))
        def _():
            copy_of(i, down, right).start()

    for i, (down, right) in enumerate(SIDES):
        has_source = inside(row - down, col - right)

        @pl.when(jnp.logical_not(has_source))
        def _():
            landings[i][...] = jnp.zeros(landings[i].shape, jnp.float32)

    for i, (down, right) in enumerate(SIDES):

        @pl.when(inside(row - down, col - right))
        def _():
            copy_of(i, -down, -right).wait_recv()

    for i, (down, right) in enumerate(SIDES):

        @pl.when(inside(row + down, col + right))
        def _():
            copy_of(i, down, right).wait_send()


def halo_kernel(field_ref, *refs):
    sources = [
        field_ref.at[:, edge(side[0], TILE), edge(side[1], TILE)] for side in SIDES
    ]
    exchange(sources, refs[:8], refs[8], refs[9])


def gradient_kernel(
    planes, offs, cnt, own, *refs
):
    halos = refs[:8]
    probe, amps, table = refs[8:11]
    center_out = refs[11]
    outs = refs[12:20]
    ext, canvas, left_m, right_m, wave, half, full = refs[20:]

    real, imag = table[0], table[1]
    left_m[:TILE, :TILE] = real
    left_m[:TILE, TILE:] = -imag
    left_m[TILE:, :TILE] = imag
    left_m[TILE:, TILE:] = real
    right_m[:TILE, :TILE] = real
    right_m[:TILE, TILE:] = imag
    right_m[TILE:, :TILE] = -imag
    right_m[TILE:, TILE:] = real

    canvas[...] = jnp.zeros_like(canvas)
    ext[:, 4] = jnp.zeros_like(ext[:, 4])
    for block in range(2):
        ext[:, 1 + block, RIM : RIM + TILE, :] = own[:, :, block * LANES : (block + 1) * LANES]
    for (down, right), halo in zip(SIDES, halos):
        rows = zone(-down)
        if right == 0:
            ext[:, 1, rows, :] = halo[:, :, :LANES]
            ext[:, 2, rows, :] = halo[:, :, LANES:]
        else:
            ext[:, 3 if right < 0 else 0, rows, :] = halo[...]

    lane = lax.broadcasted_iota(jnp.int32, (CHUNK, LANES), 1)

    def one_slot(slot, carry):
        top = offs[slot, 0]
        left = offs[slot, 1]
        first = left // LANES
        shift = left % LANES
        back = (LANES - shift) % LANES
        keep = lane < LANES - shift
        late = lane >= shift
        for at in range(0, TILE, CHUNK):
            rows = pl.ds(top + at, CHUNK)
            parts = []
            for p in range(2):
                rolled = [
                    pltpu.roll(ext[p, first + b, rows, :], back, 1) for b in range(3)
                ]
                parts.append([jnp.where(keep, rolled[b], rolled[b + 1]) for b in range(2)])
            for b in range(2):
                cols = slice(b * LANES, (b + 1) * LANES)
                pr = probe[0, at : at + CHUNK, cols]
                pi = probe[1, at : at + CHUNK, cols]
                wr, wi = parts[0][b], parts[1][b]
                wave[at : at + CHUNK, cols] = (pr * wr - pi * wi).astype(jnp.bfloat16)
                wave[TILE + at : TILE + at + CHUNK, cols] = (pr * wi + pi * wr).astype(jnp.bfloat16)

        def by_rows(matrix):
            product = jnp.dot(matrix[...], wave[...], preferred_element_type=jnp.float32)
            half[:, :TILE] = product[:TILE].astype(jnp.bfloat16)
            half[:, TILE:] = product[TILE:].astype(jnp.bfloat16)

        def by_cols(matrix):
            full[...] = jnp.dot(half[...], matrix[...], preferred_element_type=jnp.float32)

        by_rows(left_m)
        by_cols(right_m)
        for at in range(0, TILE, CHUNK):
            sr = full[at : at + CHUNK, :TILE]
            si = full[at : at + CHUNK, TILE:]
            amp = amps[slot, at : at + CHUNK, :].astype(jnp.float32)
            factor = 1.0 - amp * lax.rsqrt(sr * sr + si * si + smooth_term)
            wave[at : at + CHUNK, :] = (sr * factor).astype(jnp.bfloat16)
            wave[TILE + at : TILE + at + CHUNK, :] = (si * factor).astype(jnp.bfloat16)
        by_rows(right_m)
        by_cols(left_m)
        for at in range(0, TILE, CHUNK):
            rows = pl.ds(top + at, CHUNK)
            pieces = [[] for _ in range(planes)]
            for b in range(2):
                cols = slice(b * LANES, (b + 1) * LANES)
                pr = probe[0, at : at + CHUNK, cols]
                pi = probe[1, at : at + CHUNK, cols]
                br = full[at : at + CHUNK, cols]
                bi = full[at : at + CHUNK, TILE + b * LANES : TILE + (b + 1) * LANES]
                pieces[0].append(pltpu.roll(pr * br + pi * bi, shift, 1))
                pieces[1].append(pltpu.roll(pr * bi - pi * br, shift, 1))
                if planes > 2:
                    pieces[2].append(pltpu.roll(pr * pr + pi * pi, shift, 1))
            for p in range(planes):
                a, b = pieces[p]
                canvas[p, first, rows, :] += jnp.where(late, a, 0.0)
                canvas[p, first + 1, rows, :] += jnp.where(late, b, a)
                canvas[p, first + 2, rows, :] += jnp.where(late, 0.0, b)
        return carry

    lax.fori_loop(0, cnt[0], one_slot, 0)

    center_out[:, :, :LANES] = canvas[:, 1, RIM : RIM + TILE, :]
    center_out[:, :, LANES:] = canvas[:, 2, RIM : RIM + TILE, :]
    for (down, right), out in zip(SIDES, outs):
        rows = zone(down)
        if right == 0:
            out[:, :, :LANES] = canvas[:, 1, rows, :]
            out[:, :, LANES:] = canvas[:, 2, rows, :]
        else:
            out[...] = canvas[:, 0 if right < 0 else 3, rows, :]


def update_kernel(first, own, center, *refs):
    pieces = refs[:8]
    refs = refs[8:]
    if not first:
        scale_in = refs[0]
        refs = refs[1:]
    new = refs[0]
    landed = refs[-11:-3]
    total, sends, receives = refs[-3:]
    exchange(pieces, landed, sends, receives)
    total[...] = center[...]
    for (down, right), piece in zip(SIDES, landed):
        total[:, edge(-down, TILE), edge(-right, TILE)] += piece[...]
    if first:
        scale = step_size / (total[2] + regular_term)
        refs[1][...] = scale
    else:
        scale = scale_in[...]
    for p in range(2):
        new[p] = own[p] - total[p] * scale


def vmem(count):
    return [pl.BlockSpec(memory_space=pltpu.VMEM)] * count


def dma_sems():
    return [pltpu.SemaphoreType.DMA((8,))] * 2


def f32(shape):
    return jax.ShapeDtypeStruct(shape, jnp.float32)


def per_device(object_field, probe_field, amplitudes, offsets, counts):
    table = jnp.asarray(dft_tables())
    offs = offsets.reshape(MAXPOS, 2)
    cnt = counts.reshape(1)
    amps = amplitudes.reshape(MAXPOS, TILE, TILE)
    field = object_field
    edge_shapes = [f32(shape_of(2, side)) for side in SIDES]
    scale = None
    for iteration in range(ITERS):
        first = iteration == 0
        planes = 3 if first else 2
        halos = pl.pallas_call(
            halo_kernel,
            out_shape=edge_shapes,
            in_specs=vmem(1),
            out_specs=vmem(8),
            scratch_shapes=dma_sems(),
            compiler_params=pltpu.CompilerParams(collective_id=0, has_side_effects=True),
            name="halo",
        )(field)
        center, *pieces = pl.pallas_call(
            functools.partial(gradient_kernel, planes),
            out_shape=[f32((planes, TILE, TILE))] + [f32(shape_of(planes, s)) for s in SIDES],
            in_specs=[pl.BlockSpec(memory_space=pltpu.SMEM)] * 2 + vmem(12),
            out_specs=vmem(9),
            scratch_shapes=[
                pltpu.VMEM((2, 5, 2 * TILE, LANES), jnp.float32),
                pltpu.VMEM((planes, 5, 2 * TILE, LANES), jnp.float32),
                pltpu.VMEM((2 * TILE, 2 * TILE), jnp.bfloat16),
                pltpu.VMEM((2 * TILE, 2 * TILE), jnp.bfloat16),
                pltpu.VMEM((2 * TILE, TILE), jnp.bfloat16),
                pltpu.VMEM((TILE, 2 * TILE), jnp.bfloat16),
                pltpu.VMEM((TILE, 2 * TILE), jnp.float32),
            ],
            name=f"gradient{iteration}",
        )(offs, cnt, field, *halos, probe_field, amps, table)
        operands = [field, center, *pieces] + ([] if first else [scale])
        shapes = [f32((2, TILE, TILE))]
        if first:
            shapes.append(f32((TILE, TILE)))
        results = pl.pallas_call(
            functools.partial(update_kernel, first),
            out_shape=shapes,
            in_specs=vmem(len(operands)),
            out_specs=vmem(len(shapes)),
            scratch_shapes=[pltpu.VMEM(shape_of(planes, s), jnp.float32) for s in SIDES]
            + [pltpu.VMEM((planes, TILE, TILE), jnp.float32)]
            + dma_sems(),
            compiler_params=pltpu.CompilerParams(
                collective_id=1 + iteration, has_side_effects=True
            ),
            name=f"update{iteration}",
        )(*operands)
        field = results[0]
        if first:
            scale = results[1]
    return field


def solution(mesh):
    in_specs = (
        P(None, "row", "col"),
        P(),
        P("row", "col", None, None, None),
        P("row", "col", None, None),
        P("row", "col"),
    )
    out_specs = P(None, "row", "col")
    return jax.shard_map(
        per_device, mesh=mesh, in_specs=in_specs, out_specs=out_specs, check_vma=False
    )
```

```python
import functools
import math

import jax
import jax.numpy as jnp
import numpy as np
from jax import lax
from jax.experimental import pallas as pl
from jax.experimental.pallas import tpu as pltpu
from jax.sharding import PartitionSpec as P

TILE = 256
RIM = 128
MAXPOS = 6
ITERS = 2
LANES = 128
CHUNK = 64
VMEM_LIMIT = 28 * 1024 * 1024

smooth_term = 0.25
step_size = 0.5
regular_term = 1.0

AXES = ("row", "col")
SIDES = [(-1, 0), (1, 0), (0, -1), (0, 1), (-1, -1), (-1, 1), (1, -1), (1, 1)]


def dft_tables():
    positions = np.arange(TILE)
    phase_step = (positions[:, None] * positions[None, :]) % TILE
    angle = phase_step.astype(np.float32) * np.float32(2.0 * math.pi / TILE)
    scale = np.float32(1.0 / math.sqrt(TILE))
    real = np.cos(angle).astype(np.float32) * scale
    imag = -np.sin(angle).astype(np.float32) * scale
    return np.stack([real, imag]).astype(jnp.bfloat16)


def edge(step, length):
    if step < 0:
        return slice(0, RIM)
    if step > 0:
        return slice(length - RIM, length)
    return slice(0, length)


def zone(step):
    return (slice(0, RIM), slice(RIM, RIM + TILE), slice(RIM + TILE, 2 * RIM + TILE))[step + 1]


def shape_of(planes, side):
    return (planes, TILE if side[0] == 0 else RIM, TILE if side[1] == 0 else RIM)


def inside(row, col):
    rows, cols = lax.axis_size("row"), lax.axis_size("col")
    return (row >= 0) & (row < rows) & (col >= 0) & (col < cols)


def greet(row, col):
    barrier = pltpu.get_barrier_semaphore()
    peers = 0
    for down, right in SIDES[:4]:
        present = inside(row + down, col + right)
        peers = peers + jnp.where(present, 1, 0)

        @pl.when(present)
        def _():
            pl.semaphore_signal(
                barrier,
                inc=1,
                device_id=(row + down, col + right),
                device_id_type=pl.DeviceIdType.MESH,
            )

    pl.semaphore_wait(barrier, peers)


def transfer(source, landing, sends, receives, slot, device):
    return pltpu.make_async_remote_copy(
        src_ref=source,
        dst_ref=landing,
        send_sem=sends.at[slot],
        recv_sem=receives.at[slot],
        device_id=device,
        device_id_type=pl.DeviceIdType.MESH,
    )


def half_of(right):
    return slice(0, LANES) if right < 0 else slice(LANES, 2 * LANES)


def half_slot(down, right):
    return (0 if down < 0 else 1) + (0 if right < 0 else 8)


CORNERS = SIDES[4:]


def halo_kernel(field, *refs):
    outs = refs[:8]
    sends, receives = refs[8:]
    row, col = lax.axis_index("row"), lax.axis_index("col")
    greet(row, col)

    def row_copy(down, right, device):
        half = half_of(right)
        return transfer(
            field.at[:, edge(down, TILE), half],
            outs[SIDES.index((down, 0))].at[:, :, half],
            sends,
            receives,
            half_slot(down, right),
            device,
        )

    def col_copy(right, device):
        at = SIDES.index((0, right))
        return transfer(
            field.at[:, :, edge(right, TILE)], outs[at], sends, receives, at, device
        )

    def corner_copy(down, right, device):
        at = SIDES.index((down, right))
        landed = outs[SIDES.index((down, 0))].at[:, :, half_of(right)]
        return transfer(landed, outs[at], sends, receives, at, device)

    for down, right in CORNERS:

        @pl.when(inside(row + down, col))
        def _():
            row_copy(down, right, (row + down, col)).start()

    for right in (-1, 1):

        @pl.when(inside(row, col + right))
        def _():
            col_copy(right, (row, col + right)).start()

    for (down, right), out in zip(SIDES, outs):

        @pl.when(jnp.logical_not(inside(row - down, col - right)))
        def _():
            out[...] = jnp.zeros(out.shape, jnp.float32)

    for down, right in CORNERS:

        @pl.when(inside(row - down, col))
        def _():
            row_copy(down, right, (row - down, col)).wait_recv()

        @pl.when(inside(row - down, col) & inside(row, col + right))
        def _():
            corner_copy(down, right, (row, col + right)).start()

    for right in (-1, 1):

        @pl.when(inside(row, col - right))
        def _():
            col_copy(right, (row, col - right)).wait_recv()

    for down, right in CORNERS:

        @pl.when(inside(row - down, col - right))
        def _():
            corner_copy(down, right, (row, col - right)).wait_recv()

    for down, right in CORNERS:

        @pl.when(inside(row + down, col))
        def _():
            row_copy(down, right, (row + down, col)).wait_send()

        @pl.when(inside(row - down, col) & inside(row, col + right))
        def _():
            corner_copy(down, right, (row, col + right)).wait_send()

    for right in (-1, 1):

        @pl.when(inside(row, col + right))
        def _():
            col_copy(right, (row, col + right)).wait_send()


def gradient_kernel(
    planes, offs, cnt, own, *refs
):
    halos = refs[:8]
    probe, amps, table = refs[8:11]
    center_out = refs[11]
    outs = refs[12:20]
    ext, canvas, left_m, right_m, wave, half, full = refs[20:]

    real, imag = table[0], table[1]
    left_m[:TILE, :TILE] = real
    left_m[:TILE, TILE:] = -imag
    left_m[TILE:, :TILE] = imag
    left_m[TILE:, TILE:] = real
    right_m[:TILE, :TILE] = real
    right_m[:TILE, TILE:] = imag
    right_m[TILE:, :TILE] = -imag
    right_m[TILE:, TILE:] = real

    canvas[...] = jnp.zeros_like(canvas)
    ext[:, 4] = jnp.zeros_like(ext[:, 4])
    for block in range(2):
        ext[:, 1 + block, RIM : RIM + TILE, :] = own[:, :, block * LANES : (block + 1) * LANES]
    for (down, right), halo in zip(SIDES, halos):
        rows = zone(-down)
        if right == 0:
            ext[:, 1, rows, :] = halo[:, :, :LANES]
            ext[:, 2, rows, :] = halo[:, :, LANES:]
        else:
            ext[:, 3 if right < 0 else 0, rows, :] = halo[...]

    lane = lax.broadcasted_iota(jnp.int32, (CHUNK, LANES), 1)

    def one_slot(slot, carry):
        top = offs[slot, 0]
        left = offs[slot, 1]
        first = left // LANES
        shift = left % LANES
        back = (LANES - shift) % LANES
        keep = lane < LANES - shift
        late = lane >= shift
        for at in range(0, TILE, CHUNK):
            rows = pl.ds(top + at, CHUNK)
            parts = []
            for p in range(2):
                rolled = [
                    pltpu.roll(ext[p, first + b, rows, :], back, 1) for b in range(3)
                ]
                parts.append([jnp.where(keep, rolled[b], rolled[b + 1]) for b in range(2)])
            for b in range(2):
                cols = slice(b * LANES, (b + 1) * LANES)
                pr = probe[0, at : at + CHUNK, cols]
                pi = probe[1, at : at + CHUNK, cols]
                wr, wi = parts[0][b], parts[1][b]
                wave[at : at + CHUNK, cols] = (pr * wr - pi * wi).astype(jnp.bfloat16)
                wave[TILE + at : TILE + at + CHUNK, cols] = (pr * wi + pi * wr).astype(jnp.bfloat16)

        def by_rows(matrix):
            product = jnp.dot(matrix[...], wave[...], preferred_element_type=jnp.float32)
            half[:, :TILE] = product[:TILE].astype(jnp.bfloat16)
            half[:, TILE:] = product[TILE:].astype(jnp.bfloat16)

        def by_cols(matrix):
            full[...] = jnp.dot(half[...], matrix[...], preferred_element_type=jnp.float32)

        by_rows(left_m)
        by_cols(right_m)
        for at in range(0, TILE, CHUNK):
            sr = full[at : at + CHUNK, :TILE]
            si = full[at : at + CHUNK, TILE:]
            amp = amps[slot, at : at + CHUNK, :].astype(jnp.float32)
            factor = 1.0 - amp * lax.rsqrt(sr * sr + si * si + smooth_term)
            wave[at : at + CHUNK, :] = (sr * factor).astype(jnp.bfloat16)
            wave[TILE + at : TILE + at + CHUNK, :] = (si * factor).astype(jnp.bfloat16)
        by_rows(right_m)
        by_cols(left_m)
        for at in range(0, TILE, CHUNK):
            rows = pl.ds(top + at, CHUNK)
            pieces = [[] for _ in range(planes)]
            for b in range(2):
                cols = slice(b * LANES, (b + 1) * LANES)
                pr = probe[0, at : at + CHUNK, cols]
                pi = probe[1, at : at + CHUNK, cols]
                br = full[at : at + CHUNK, cols]
                bi = full[at : at + CHUNK, TILE + b * LANES : TILE + (b + 1) * LANES]
                pieces[0].append(pltpu.roll(pr * br + pi * bi, shift, 1))
                pieces[1].append(pltpu.roll(pr * bi - pi * br, shift, 1))
                if planes > 2:
                    pieces[2].append(pltpu.roll(pr * pr + pi * pi, shift, 1))
            for p in range(planes):
                a, b = pieces[p]
                canvas[p, first, rows, :] += jnp.where(late, a, 0.0)
                canvas[p, first + 1, rows, :] += jnp.where(late, b, a)
                canvas[p, first + 2, rows, :] += jnp.where(late, 0.0, b)
        return carry

    lax.fori_loop(0, cnt[0], one_slot, 0)

    center_out[:, :, :LANES] = canvas[:, 1, RIM : RIM + TILE, :]
    center_out[:, :, LANES:] = canvas[:, 2, RIM : RIM + TILE, :]
    for (down, right), out in zip(SIDES, outs):
        rows = zone(down)
        if right == 0:
            out[:, :, :LANES] = canvas[:, 1, rows, :]
            out[:, :, LANES:] = canvas[:, 2, rows, :]
        else:
            out[...] = canvas[:, 0 if right < 0 else 3, rows, :]


def update_kernel(first, own, center, *refs):
    pieces = refs[:8]
    refs = refs[8:]
    if not first:
        scale_in = refs[0]
        refs = refs[1:]
    new = refs[0]
    landed = refs[-13:-5]
    sums = refs[-5:-3]
    total, sends, receives = refs[-3:]
    row, col = lax.axis_index("row"), lax.axis_index("col")
    greet(row, col)

    def corner_copy(down, right, device):
        at = SIDES.index((down, right))
        return transfer(pieces[at], landed[at], sends, receives, at, device)

    def col_copy(right, device):
        at = SIDES.index((0, right))
        return transfer(pieces[at], landed[at], sends, receives, at, device)

    def row_copy(down, right, device):
        at = SIDES.index((down, 0))
        half = half_of(right)
        return transfer(
            sums[at].at[:, :, half],
            landed[at].at[:, :, half],
            sends,
            receives,
            half_slot(down, right),
            device,
        )

    for down, right in CORNERS:

        @pl.when(inside(row + down, col + right))
        def _():
            corner_copy(down, right, (row, col + right)).start()

    for right in (-1, 1):

        @pl.when(inside(row, col + right))
        def _():
            col_copy(right, (row, col + right)).start()

    for at, (down, right) in enumerate(SIDES[:4]):

        @pl.when(jnp.logical_not(inside(row - down, col - right)))
        def _():
            landed[at][...] = jnp.zeros(landed[at].shape, jnp.float32)

    for at in range(2):
        sums[at][...] = pieces[at][...]
    for down, right in CORNERS:

        @pl.when(inside(row + down, col) & inside(row, col - right))
        def _():
            corner_copy(down, right, (row, col - right)).wait_recv()
            at = SIDES.index((down, 0))
            sums[at][:, :, half_of(-right)] += landed[SIDES.index((down, right))][...]

    total[...] = center[...]
    for down, right in CORNERS:

        @pl.when(inside(row + down, col))
        def _():
            row_copy(down, right, (row + down, col)).start()

    for right in (-1, 1):

        @pl.when(inside(row, col - right))
        def _():
            col_copy(right, (row, col - right)).wait_recv()

        total[:, :, edge(-right, TILE)] += landed[SIDES.index((0, right))][...]

    for down, right in CORNERS:

        @pl.when(inside(row - down, col))
        def _():
            row_copy(down, right, (row - down, col)).wait_recv()

    for down in (-1, 1):
        total[:, edge(-down, TILE), :] += landed[SIDES.index((down, 0))][...]

    for down, right in CORNERS:

        @pl.when(inside(row + down, col + right))
        def _():
            corner_copy(down, right, (row, col + right)).wait_send()

        @pl.when(inside(row + down, col))
        def _():
            row_copy(down, right, (row + down, col)).wait_send()

    for right in (-1, 1):

        @pl.when(inside(row, col + right))
        def _():
            col_copy(right, (row, col + right)).wait_send()

    if first:
        scale = step_size / (total[2] + regular_term)
        refs[1][...] = scale
    else:
        scale = scale_in[...]
    for p in range(2):
        new[p] = own[p] - total[p] * scale


def vmem(count):
    return [pl.BlockSpec(memory_space=pltpu.VMEM)] * count


def dma_sems():
    return [pltpu.SemaphoreType.DMA((10,))] * 2


def f32(shape):
    return jax.ShapeDtypeStruct(shape, jnp.float32)


def per_device(object_field, probe_field, amplitudes, offsets, counts):
    table = jnp.asarray(dft_tables())
    offs = offsets.reshape(MAXPOS, 2)
    cnt = counts.reshape(1)
    amps = amplitudes.reshape(MAXPOS, TILE, TILE)
    field = object_field
    edge_shapes = [f32(shape_of(2, side)) for side in SIDES]
    scale = None
    for iteration in range(ITERS):
        first = iteration == 0
        planes = 3 if first else 2
        halos = pl.pallas_call(
            halo_kernel,
            out_shape=edge_shapes,
            in_specs=vmem(1),
            out_specs=vmem(8),
            scratch_shapes=dma_sems(),
            compiler_params=pltpu.CompilerParams(collective_id=0, has_side_effects=True, vmem_limit_bytes=VMEM_LIMIT),
            name="halo",
        )(field)
        center, *pieces = pl.pallas_call(
            functools.partial(gradient_kernel, planes),
            out_shape=[f32((planes, TILE, TILE))] + [f32(shape_of(planes, s)) for s in SIDES],
            in_specs=[pl.BlockSpec(memory_space=pltpu.SMEM)] * 2 + vmem(12),
            out_specs=vmem(9),
            scratch_shapes=[
                pltpu.VMEM((2, 5, 2 * TILE, LANES), jnp.float32),
                pltpu.VMEM((planes, 5, 2 * TILE, LANES), jnp.float32),
                pltpu.VMEM((2 * TILE, 2 * TILE), jnp.bfloat16),
                pltpu.VMEM((2 * TILE, 2 * TILE), jnp.bfloat16),
                pltpu.VMEM((2 * TILE, TILE), jnp.bfloat16),
                pltpu.VMEM((TILE, 2 * TILE), jnp.bfloat16),
                pltpu.VMEM((TILE, 2 * TILE), jnp.float32),
            ],
            compiler_params=pltpu.CompilerParams(vmem_limit_bytes=VMEM_LIMIT),
            name=f"gradient{iteration}",
        )(offs, cnt, field, *halos, probe_field, amps, table)
        operands = [field, center, *pieces] + ([] if first else [scale])
        shapes = [f32((2, TILE, TILE))]
        if first:
            shapes.append(f32((TILE, TILE)))
        results = pl.pallas_call(
            functools.partial(update_kernel, first),
            out_shape=shapes,
            in_specs=vmem(len(operands)),
            out_specs=vmem(len(shapes)),
            scratch_shapes=[pltpu.VMEM(shape_of(planes, s), jnp.float32) for s in SIDES]
            + [pltpu.VMEM((planes, RIM, TILE), jnp.float32)] * 2
            + [pltpu.VMEM((planes, TILE, TILE), jnp.float32)]
            + dma_sems(),
            compiler_params=pltpu.CompilerParams(
                collective_id=1 + iteration,
                has_side_effects=True,
                vmem_limit_bytes=VMEM_LIMIT,
            ),
            name=f"update{iteration}",
        )(*operands)
        field = results[0]
        if first:
            scale = results[1]
    return field


def solution(mesh):
    in_specs = (
        P(None, "row", "col"),
        P(),
        P("row", "col", None, None, None),
        P("row", "col", None, None),
        P("row", "col"),
    )
    out_specs = P(None, "row", "col")
    return jax.shard_map(
        per_device, mesh=mesh, in_specs=in_specs, out_specs=out_specs, check_vma=False
    )
```

```python
import functools
import math

import jax
import jax.numpy as jnp
import numpy as np
from jax import lax
from jax.experimental import pallas as pl
from jax.experimental.pallas import tpu as pltpu
from jax.sharding import PartitionSpec as P

TILE = 256
RIM = 128
MAXPOS = 6
ITERS = 2
LANES = 128
CHUNK = 64
VMEM_LIMIT = 28 * 1024 * 1024
WIRE_COST = pl.CostEstimate(flops=0, transcendentals=0, bytes_accessed=40_000_000)

smooth_term = 0.25
step_size = 0.5
regular_term = 1.0

AXES = ("row", "col")
SIDES = [(-1, 0), (1, 0), (0, -1), (0, 1), (-1, -1), (-1, 1), (1, -1), (1, 1)]


def dft_tables():
    positions = np.arange(TILE)
    phase_step = (positions[:, None] * positions[None, :]) % TILE
    angle = phase_step.astype(np.float32) * np.float32(2.0 * math.pi / TILE)
    scale = np.float32(1.0 / math.sqrt(TILE))
    real = np.cos(angle).astype(np.float32) * scale
    imag = -np.sin(angle).astype(np.float32) * scale
    return np.stack([real, imag]).astype(jnp.bfloat16)


def edge(step, length):
    if step < 0:
        return slice(0, RIM)
    if step > 0:
        return slice(length - RIM, length)
    return slice(0, length)


def zone(step):
    return (slice(0, RIM), slice(RIM, RIM + TILE), slice(RIM + TILE, 2 * RIM + TILE))[step + 1]


def shape_of(planes, side):
    return (planes, TILE if side[0] == 0 else RIM, TILE if side[1] == 0 else RIM)


def inside(row, col):
    rows, cols = lax.axis_size("row"), lax.axis_size("col")
    return (row >= 0) & (row < rows) & (col >= 0) & (col < cols)


def greet(row, col):
    barrier = pltpu.get_barrier_semaphore()
    peers = 0
    for down, right in SIDES[:4]:
        present = inside(row + down, col + right)
        peers = peers + jnp.where(present, 1, 0)

        @pl.when(present)
        def _():
            pl.semaphore_signal(
                barrier,
                inc=1,
                device_id=(row + down, col + right),
                device_id_type=pl.DeviceIdType.MESH,
            )

    pl.semaphore_wait(barrier, peers)


def transfer(source, landing, sends, receives, slot, device):
    return pltpu.make_async_remote_copy(
        src_ref=source,
        dst_ref=landing,
        send_sem=sends.at[slot],
        recv_sem=receives.at[slot],
        device_id=device,
        device_id_type=pl.DeviceIdType.MESH,
    )


def half_of(right):
    return slice(0, LANES) if right < 0 else slice(LANES, 2 * LANES)


def half_slot(down, right):
    return (0 if down < 0 else 1) + (0 if right < 0 else 8)


CORNERS = SIDES[4:]


def halo_kernel(field, *refs):
    outs = refs[:8]
    sends, receives = refs[8:]
    row, col = lax.axis_index("row"), lax.axis_index("col")
    greet(row, col)

    def row_copy(down, right, device):
        half = half_of(right)
        return transfer(
            field.at[:, edge(down, TILE), half],
            outs[SIDES.index((down, 0))].at[:, :, half],
            sends,
            receives,
            half_slot(down, right),
            device,
        )

    def col_copy(right, device):
        at = SIDES.index((0, right))
        return transfer(
            field.at[:, :, edge(right, TILE)], outs[at], sends, receives, at, device
        )

    def corner_copy(down, right, device):
        at = SIDES.index((down, right))
        landed = outs[SIDES.index((down, 0))].at[:, :, half_of(right)]
        return transfer(landed, outs[at], sends, receives, at, device)

    for down, right in CORNERS:

        @pl.when(inside(row + down, col))
        def _():
            row_copy(down, right, (row + down, col)).start()

    for right in (-1, 1):

        @pl.when(inside(row, col + right))
        def _():
            col_copy(right, (row, col + right)).start()

    for (down, right), out in zip(SIDES, outs):

        @pl.when(jnp.logical_not(inside(row - down, col - right)))
        def _():
            out[...] = jnp.zeros(out.shape, jnp.float32)

    for down, right in CORNERS:

        @pl.when(inside(row - down, col))
        def _():
            row_copy(down, right, (row - down, col)).wait_recv()

        @pl.when(inside(row - down, col) & inside(row, col + right))
        def _():
            corner_copy(down, right, (row, col + right)).start()

    for right in (-1, 1):

        @pl.when(inside(row, col - right))
        def _():
            col_copy(right, (row, col - right)).wait_recv()

    for down, right in CORNERS:

        @pl.when(inside(row - down, col - right))
        def _():
            corner_copy(down, right, (row, col - right)).wait_recv()

    for down, right in CORNERS:

        @pl.when(inside(row + down, col))
        def _():
            row_copy(down, right, (row + down, col)).wait_send()

        @pl.when(inside(row - down, col) & inside(row, col + right))
        def _():
            corner_copy(down, right, (row, col + right)).wait_send()

    for right in (-1, 1):

        @pl.when(inside(row, col + right))
        def _():
            col_copy(right, (row, col + right)).wait_send()


def gradient_kernel(
    planes, offs, cnt, own, *refs
):
    halos = refs[:8]
    probe, amps, table = refs[8:11]
    center_out = refs[11]
    outs = refs[12:20]
    ext, canvas, left_m, right_m, wave, half, full = refs[20:]

    real, imag = table[0], table[1]
    left_m[:TILE, :TILE] = real
    left_m[:TILE, TILE:] = -imag
    left_m[TILE:, :TILE] = imag
    left_m[TILE:, TILE:] = real
    right_m[:TILE, :TILE] = real
    right_m[:TILE, TILE:] = imag
    right_m[TILE:, :TILE] = -imag
    right_m[TILE:, TILE:] = real

    canvas[...] = jnp.zeros_like(canvas)
    ext[:, 4] = jnp.zeros_like(ext[:, 4])
    for block in range(2):
        ext[:, 1 + block, RIM : RIM + TILE, :] = own[:, :, block * LANES : (block + 1) * LANES]
    for (down, right), halo in zip(SIDES, halos):
        rows = zone(-down)
        if right == 0:
            ext[:, 1, rows, :] = halo[:, :, :LANES]
            ext[:, 2, rows, :] = halo[:, :, LANES:]
        else:
            ext[:, 3 if right < 0 else 0, rows, :] = halo[...]

    lane = lax.broadcasted_iota(jnp.int32, (CHUNK, LANES), 1)

    def one_slot(slot, carry):
        top = offs[0, slot]
        left = offs[1, slot]
        first = left // LANES
        shift = left % LANES
        back = (LANES - shift) % LANES
        keep = lane < LANES - shift
        late = lane >= shift
        for at in range(0, TILE, CHUNK):
            rows = pl.ds(top + at, CHUNK)
            parts = []
            for p in range(2):
                rolled = [
                    pltpu.roll(ext[p, first + b, rows, :], back, 1) for b in range(3)
                ]
                parts.append([jnp.where(keep, rolled[b], rolled[b + 1]) for b in range(2)])
            for b in range(2):
                cols = slice(b * LANES, (b + 1) * LANES)
                pr = probe[0, at : at + CHUNK, cols]
                pi = probe[1, at : at + CHUNK, cols]
                wr, wi = parts[0][b], parts[1][b]
                wave[at : at + CHUNK, cols] = (pr * wr - pi * wi).astype(jnp.bfloat16)
                wave[TILE + at : TILE + at + CHUNK, cols] = (pr * wi + pi * wr).astype(jnp.bfloat16)

        def by_rows(matrix):
            product = jnp.dot(matrix[...], wave[...], preferred_element_type=jnp.float32)
            half[:, :TILE] = product[:TILE].astype(jnp.bfloat16)
            half[:, TILE:] = product[TILE:].astype(jnp.bfloat16)

        def by_cols(matrix):
            full[...] = jnp.dot(half[...], matrix[...], preferred_element_type=jnp.float32)

        by_rows(left_m)
        by_cols(right_m)
        for at in range(0, TILE, CHUNK):
            sr = full[at : at + CHUNK, :TILE]
            si = full[at : at + CHUNK, TILE:]
            amp = amps[slot, at : at + CHUNK, :].astype(jnp.float32)
            factor = 1.0 - amp * lax.rsqrt(sr * sr + si * si + smooth_term)
            wave[at : at + CHUNK, :] = (sr * factor).astype(jnp.bfloat16)
            wave[TILE + at : TILE + at + CHUNK, :] = (si * factor).astype(jnp.bfloat16)
        by_rows(right_m)
        by_cols(left_m)
        for at in range(0, TILE, CHUNK):
            rows = pl.ds(top + at, CHUNK)
            pieces = [[] for _ in range(planes)]
            for b in range(2):
                cols = slice(b * LANES, (b + 1) * LANES)
                pr = probe[0, at : at + CHUNK, cols]
                pi = probe[1, at : at + CHUNK, cols]
                br = full[at : at + CHUNK, cols]
                bi = full[at : at + CHUNK, TILE + b * LANES : TILE + (b + 1) * LANES]
                pieces[0].append(pltpu.roll(pr * br + pi * bi, shift, 1))
                pieces[1].append(pltpu.roll(pr * bi - pi * br, shift, 1))
                if planes > 2:
                    pieces[2].append(pltpu.roll(pr * pr + pi * pi, shift, 1))
            for p in range(planes):
                a, b = pieces[p]
                canvas[p, first, rows, :] += jnp.where(late, a, 0.0)
                canvas[p, first + 1, rows, :] += jnp.where(late, b, a)
                canvas[p, first + 2, rows, :] += jnp.where(late, 0.0, b)
        return carry

    lax.fori_loop(0, cnt[0], one_slot, 0)

    center_out[:, :, :LANES] = canvas[:, 1, RIM : RIM + TILE, :]
    center_out[:, :, LANES:] = canvas[:, 2, RIM : RIM + TILE, :]
    for (down, right), out in zip(SIDES, outs):
        rows = zone(down)
        if right == 0:
            out[:, :, :LANES] = canvas[:, 1, rows, :]
            out[:, :, LANES:] = canvas[:, 2, rows, :]
        else:
            out[...] = canvas[:, 0 if right < 0 else 3, rows, :]


def update_kernel(first, own, center, *refs):
    pieces = refs[:8]
    refs = refs[8:]
    if not first:
        scale_in = refs[0]
        refs = refs[1:]
    new = refs[0]
    landed = refs[-13:-5]
    sums = refs[-5:-3]
    total, sends, receives = refs[-3:]
    row, col = lax.axis_index("row"), lax.axis_index("col")
    greet(row, col)

    def corner_copy(down, right, device):
        at = SIDES.index((down, right))
        return transfer(pieces[at], landed[at], sends, receives, at, device)

    def col_copy(right, device):
        at = SIDES.index((0, right))
        return transfer(pieces[at], landed[at], sends, receives, at, device)

    def row_copy(down, right, device):
        at = SIDES.index((down, 0))
        half = half_of(right)
        return transfer(
            sums[at].at[:, :, half],
            landed[at].at[:, :, half],
            sends,
            receives,
            half_slot(down, right),
            device,
        )

    for down, right in CORNERS:

        @pl.when(inside(row + down, col + right))
        def _():
            corner_copy(down, right, (row, col + right)).start()

    for right in (-1, 1):

        @pl.when(inside(row, col + right))
        def _():
            col_copy(right, (row, col + right)).start()

    for at, (down, right) in enumerate(SIDES[:4]):

        @pl.when(jnp.logical_not(inside(row - down, col - right)))
        def _():
            landed[at][...] = jnp.zeros(landed[at].shape, jnp.float32)

    for at in range(2):
        sums[at][...] = pieces[at][...]
    def send_half(side):
        half = half_of(side)
        for down in (-1, 1):

            @pl.when(inside(row + down, col) & inside(row, col + side))
            def _():
                corner_copy(down, -side, (row, col + side)).wait_recv()
                landing = landed[SIDES.index((down, -side))]
                sums[SIDES.index((down, 0))][:, :, half] += landing[...]

        total[:, :, half] = center[:, :, half]
        for down in (-1, 1):

            @pl.when(inside(row + down, col))
            def _():
                row_copy(down, side, (row + down, col)).start()

    @pl.when(col % 2 == 1)
    def _():
        send_half(-1)
        send_half(1)

    @pl.when(col % 2 == 0)
    def _():
        send_half(1)
        send_half(-1)

    for right in (-1, 1):

        @pl.when(inside(row, col - right))
        def _():
            col_copy(right, (row, col - right)).wait_recv()

        total[:, :, edge(-right, TILE)] += landed[SIDES.index((0, right))][...]

    for down, right in CORNERS:

        @pl.when(inside(row - down, col))
        def _():
            row_copy(down, right, (row - down, col)).wait_recv()

    for down in (-1, 1):
        total[:, edge(-down, TILE), :] += landed[SIDES.index((down, 0))][...]

    for down, right in CORNERS:

        @pl.when(inside(row + down, col + right))
        def _():
            corner_copy(down, right, (row, col + right)).wait_send()

        @pl.when(inside(row + down, col))
        def _():
            row_copy(down, right, (row + down, col)).wait_send()

    for right in (-1, 1):

        @pl.when(inside(row, col + right))
        def _():
            col_copy(right, (row, col + right)).wait_send()

    if first:
        scale = step_size / (total[2] + regular_term)
        refs[1][...] = scale
    else:
        scale = scale_in[...]
    for p in range(2):
        new[p] = own[p] - total[p] * scale


def vmem(count):
    return [pl.BlockSpec(memory_space=pltpu.VMEM)] * count


def dma_sems():
    return [pltpu.SemaphoreType.DMA((10,))] * 2


def f32(shape):
    return jax.ShapeDtypeStruct(shape, jnp.float32)


def per_device(object_field, probe_field, amplitudes, offsets, counts):
    table = jnp.asarray(dft_tables())
    offs = offsets.reshape(MAXPOS, 2).T
    cnt = counts.reshape(1)
    amps = amplitudes.reshape(MAXPOS, TILE, TILE)
    field = object_field
    edge_shapes = [f32(shape_of(2, side)) for side in SIDES]
    scale = None
    for iteration in range(ITERS):
        first = iteration == 0
        planes = 3 if first else 2
        halos = pl.pallas_call(
            halo_kernel,
            out_shape=edge_shapes,
            in_specs=vmem(1),
            out_specs=vmem(8),
            scratch_shapes=dma_sems(),
            compiler_params=pltpu.CompilerParams(collective_id=0, has_side_effects=True, vmem_limit_bytes=VMEM_LIMIT),
            cost_estimate=WIRE_COST,
            name="halo",
        )(field)
        center, *pieces = pl.pallas_call(
            functools.partial(gradient_kernel, planes),
            out_shape=[f32((planes, TILE, TILE))] + [f32(shape_of(planes, s)) for s in SIDES],
            in_specs=[pl.BlockSpec(memory_space=pltpu.SMEM)] * 2 + vmem(12),
            out_specs=vmem(9),
            scratch_shapes=[
                pltpu.VMEM((2, 5, 2 * TILE, LANES), jnp.float32),
                pltpu.VMEM((planes, 5, 2 * TILE, LANES), jnp.float32),
                pltpu.VMEM((2 * TILE, 2 * TILE), jnp.bfloat16),
                pltpu.VMEM((2 * TILE, 2 * TILE), jnp.bfloat16),
                pltpu.VMEM((2 * TILE, TILE), jnp.bfloat16),
                pltpu.VMEM((TILE, 2 * TILE), jnp.bfloat16),
                pltpu.VMEM((TILE, 2 * TILE), jnp.float32),
            ],
            compiler_params=pltpu.CompilerParams(vmem_limit_bytes=VMEM_LIMIT),
            name=f"gradient{iteration}",
        )(offs, cnt, field, *halos, probe_field, amps, table)
        operands = [field, center, *pieces] + ([] if first else [scale])
        shapes = [f32((2, TILE, TILE))]
        if first:
            shapes.append(f32((TILE, TILE)))
        results = pl.pallas_call(
            functools.partial(update_kernel, first),
            out_shape=shapes,
            in_specs=vmem(len(operands)),
            out_specs=vmem(len(shapes)),
            scratch_shapes=[pltpu.VMEM(shape_of(planes, s), jnp.float32) for s in SIDES]
            + [pltpu.VMEM((planes, RIM, TILE), jnp.float32)] * 2
            + [pltpu.VMEM((planes, TILE, TILE), jnp.float32)]
            + dma_sems(),
            compiler_params=pltpu.CompilerParams(
                collective_id=1 + iteration,
                has_side_effects=True,
                vmem_limit_bytes=VMEM_LIMIT,
            ),
            cost_estimate=WIRE_COST,
            name=f"update{iteration}",
        )(*operands)
        field = results[0]
        if first:
            scale = results[1]
    return field


def solution(mesh):
    in_specs = (
        P(None, "row", "col"),
        P(),
        P("row", "col", None, None, None),
        P("row", "col", None, None),
        P("row", "col"),
    )
    out_specs = P(None, "row", "col")
    return jax.shard_map(
        per_device, mesh=mesh, in_specs=in_specs, out_specs=out_specs, check_vma=False
    )
```

```python
import functools
import math

import jax
import jax.numpy as jnp
import numpy as np
from jax import lax
from jax.experimental import pallas as pl
from jax.experimental.pallas import tpu as pltpu
from jax.sharding import PartitionSpec as P

TILE = 256
RIM = 128
MAXPOS = 6
ITERS = 2
LANES = 128
CHUNK = 32
VMEM_LIMIT = 28 * 1024 * 1024
WIRE_COST = pl.CostEstimate(flops=0, transcendentals=0, bytes_accessed=40_000_000)

smooth_term = 0.25
step_size = 0.5
regular_term = 1.0

AXES = ("row", "col")
SIDES = [(-1, 0), (1, 0), (0, -1), (0, 1), (-1, -1), (-1, 1), (1, -1), (1, 1)]


def dft_tables():
    positions = np.arange(TILE)
    phase_step = (positions[:, None] * positions[None, :]) % TILE
    angle = phase_step.astype(np.float32) * np.float32(2.0 * math.pi / TILE)
    scale = np.float32(1.0 / math.sqrt(TILE))
    real = np.cos(angle).astype(np.float32) * scale
    imag = -np.sin(angle).astype(np.float32) * scale
    return np.stack([real, imag]).astype(jnp.bfloat16)


def edge(step, length):
    if step < 0:
        return slice(0, RIM)
    if step > 0:
        return slice(length - RIM, length)
    return slice(0, length)


def zone(step):
    return (slice(0, RIM), slice(RIM, RIM + TILE), slice(RIM + TILE, 2 * RIM + TILE))[step + 1]


def shape_of(planes, side):
    return (planes, TILE if side[0] == 0 else RIM, TILE if side[1] == 0 else RIM)


def inside(row, col):
    rows, cols = lax.axis_size("row"), lax.axis_size("col")
    return (row >= 0) & (row < rows) & (col >= 0) & (col < cols)


def greet(row, col):
    barrier = pltpu.get_barrier_semaphore()
    peers = 0
    for down, right in SIDES[:4]:
        present = inside(row + down, col + right)
        peers = peers + jnp.where(present, 1, 0)

        @pl.when(present)
        def _():
            pl.semaphore_signal(
                barrier,
                inc=1,
                device_id=(row + down, col + right),
                device_id_type=pl.DeviceIdType.MESH,
            )

    pl.semaphore_wait(barrier, peers)


def transfer(source, landing, sends, receives, slot, device):
    return pltpu.make_async_remote_copy(
        src_ref=source,
        dst_ref=landing,
        send_sem=sends.at[slot],
        recv_sem=receives.at[slot],
        device_id=device,
        device_id_type=pl.DeviceIdType.MESH,
    )


def half_of(right):
    return slice(0, LANES) if right < 0 else slice(LANES, 2 * LANES)


def half_slot(down, right):
    return (0 if down < 0 else 1) + (0 if right < 0 else 8)


CORNERS = SIDES[4:]


def halo_kernel(field, *refs):
    outs = refs[:8]
    sends, receives = refs[8:]
    row, col = lax.axis_index("row"), lax.axis_index("col")
    greet(row, col)

    def row_copy(down, right, device):
        half = half_of(right)
        return transfer(
            field.at[:, edge(down, TILE), half],
            outs[SIDES.index((down, 0))].at[:, :, half],
            sends,
            receives,
            half_slot(down, right),
            device,
        )

    def col_copy(right, device):
        at = SIDES.index((0, right))
        return transfer(
            field.at[:, :, edge(right, TILE)], outs[at], sends, receives, at, device
        )

    def corner_copy(down, right, device):
        at = SIDES.index((down, right))
        landed = outs[SIDES.index((down, 0))].at[:, :, half_of(right)]
        return transfer(landed, outs[at], sends, receives, at, device)

    for down, right in CORNERS:

        @pl.when(inside(row + down, col))
        def _():
            row_copy(down, right, (row + down, col)).start()

    for right in (-1, 1):

        @pl.when(inside(row, col + right))
        def _():
            col_copy(right, (row, col + right)).start()

    for (down, right), out in zip(SIDES, outs):

        @pl.when(jnp.logical_not(inside(row - down, col - right)))
        def _():
            out[...] = jnp.zeros(out.shape, jnp.float32)

    for down, right in CORNERS:

        @pl.when(inside(row - down, col))
        def _():
            row_copy(down, right, (row - down, col)).wait_recv()

        @pl.when(inside(row - down, col) & inside(row, col + right))
        def _():
            corner_copy(down, right, (row, col + right)).start()

    for right in (-1, 1):

        @pl.when(inside(row, col - right))
        def _():
            col_copy(right, (row, col - right)).wait_recv()

    for down, right in CORNERS:

        @pl.when(inside(row - down, col - right))
        def _():
            corner_copy(down, right, (row, col - right)).wait_recv()

    for down, right in CORNERS:

        @pl.when(inside(row + down, col))
        def _():
            row_copy(down, right, (row + down, col)).wait_send()

        @pl.when(inside(row - down, col) & inside(row, col + right))
        def _():
            corner_copy(down, right, (row, col + right)).wait_send()

    for right in (-1, 1):

        @pl.when(inside(row, col + right))
        def _():
            col_copy(right, (row, col + right)).wait_send()


def gradient_kernel(
    planes, offs, cnt, own, *refs
):
    halos = refs[:8]
    probe, amps, table = refs[8:11]
    center_out = refs[11]
    outs = refs[12:20]
    ext, canvas, left_m, right_m, wave, half, full = refs[20:]

    real, imag = table[0], table[1]
    left_m[:TILE, :TILE] = real
    left_m[:TILE, TILE:] = -imag
    left_m[TILE:, :TILE] = imag
    left_m[TILE:, TILE:] = real
    right_m[:TILE, :TILE] = real
    right_m[:TILE, TILE:] = imag
    right_m[TILE:, :TILE] = -imag
    right_m[TILE:, TILE:] = real

    canvas[...] = jnp.zeros_like(canvas)
    ext[:, 4] = jnp.zeros_like(ext[:, 4])
    for block in range(2):
        ext[:, 1 + block, RIM : RIM + TILE, :] = own[:, :, block * LANES : (block + 1) * LANES]
    for (down, right), halo in zip(SIDES, halos):
        rows = zone(-down)
        if right == 0:
            ext[:, 1, rows, :] = halo[:, :, :LANES]
            ext[:, 2, rows, :] = halo[:, :, LANES:]
        else:
            ext[:, 3 if right < 0 else 0, rows, :] = halo[...]

    lane = lax.broadcasted_iota(jnp.int32, (CHUNK, LANES), 1)

    def one_slot(slot, carry):
        top = offs[0, slot]
        left = offs[1, slot]
        first = left // LANES
        shift = left % LANES
        back = (LANES - shift) % LANES
        keep = lane < LANES - shift
        late = lane >= shift
        for at in range(0, TILE, CHUNK):
            rows = pl.ds(top + at, CHUNK)
            parts = []
            for p in range(2):
                rolled = [
                    pltpu.roll(ext[p, first + b, rows, :], back, 1) for b in range(3)
                ]
                parts.append([jnp.where(keep, rolled[b], rolled[b + 1]) for b in range(2)])
            for b in range(2):
                cols = slice(b * LANES, (b + 1) * LANES)
                pr = probe[0, at : at + CHUNK, cols]
                pi = probe[1, at : at + CHUNK, cols]
                wr, wi = parts[0][b], parts[1][b]
                wave[at : at + CHUNK, cols] = (pr * wr - pi * wi).astype(jnp.bfloat16)
                wave[TILE + at : TILE + at + CHUNK, cols] = (pr * wi + pi * wr).astype(jnp.bfloat16)

        def by_rows(matrix):
            product = jnp.dot(matrix[...], wave[...], preferred_element_type=jnp.float32)
            half[:, :TILE] = product[:TILE].astype(jnp.bfloat16)
            half[:, TILE:] = product[TILE:].astype(jnp.bfloat16)

        def by_cols(matrix):
            full[...] = jnp.dot(half[...], matrix[...], preferred_element_type=jnp.float32)

        by_rows(left_m)
        by_cols(right_m)
        for at in range(0, TILE, CHUNK):
            sr = full[at : at + CHUNK, :TILE]
            si = full[at : at + CHUNK, TILE:]
            amp = amps[slot, at : at + CHUNK, :].astype(jnp.float32)
            factor = 1.0 - amp * lax.rsqrt(sr * sr + si * si + smooth_term)
            wave[at : at + CHUNK, :] = (sr * factor).astype(jnp.bfloat16)
            wave[TILE + at : TILE + at + CHUNK, :] = (si * factor).astype(jnp.bfloat16)
        by_rows(right_m)
        by_cols(left_m)
        for at in range(0, TILE, CHUNK):
            rows = pl.ds(top + at, CHUNK)
            pieces = [[] for _ in range(planes)]
            for b in range(2):
                cols = slice(b * LANES, (b + 1) * LANES)
                pr = probe[0, at : at + CHUNK, cols]
                pi = probe[1, at : at + CHUNK, cols]
                br = full[at : at + CHUNK, cols]
                bi = full[at : at + CHUNK, TILE + b * LANES : TILE + (b + 1) * LANES]
                pieces[0].append(pltpu.roll(pr * br + pi * bi, shift, 1))
                pieces[1].append(pltpu.roll(pr * bi - pi * br, shift, 1))
                if planes > 2:
                    pieces[2].append(pltpu.roll(pr * pr + pi * pi, shift, 1))
            for p in range(planes):
                a, b = pieces[p]
                canvas[p, first, rows, :] += jnp.where(late, a, 0.0)
                canvas[p, first + 1, rows, :] += jnp.where(late, b, a)
                canvas[p, first + 2, rows, :] += jnp.where(late, 0.0, b)
        return carry

    lax.fori_loop(0, cnt[0], one_slot, 0)

    center_out[:, :, :LANES] = canvas[:, 1, RIM : RIM + TILE, :]
    center_out[:, :, LANES:] = canvas[:, 2, RIM : RIM + TILE, :]
    for (down, right), out in zip(SIDES, outs):
        rows = zone(down)
        if right == 0:
            out[:, :, :LANES] = canvas[:, 1, rows, :]
            out[:, :, LANES:] = canvas[:, 2, rows, :]
        else:
            out[...] = canvas[:, 0 if right < 0 else 3, rows, :]


def update_kernel(first, own, center, *refs):
    pieces = refs[:8]
    refs = refs[8:]
    if not first:
        scale_in = refs[0]
        refs = refs[1:]
    new = refs[0]
    landed = refs[-13:-5]
    sums = refs[-5:-3]
    total, sends, receives = refs[-3:]
    row, col = lax.axis_index("row"), lax.axis_index("col")
    greet(row, col)

    def corner_copy(down, right, device):
        at = SIDES.index((down, right))
        return transfer(pieces[at], landed[at], sends, receives, at, device)

    def col_copy(right, device):
        at = SIDES.index((0, right))
        return transfer(pieces[at], landed[at], sends, receives, at, device)

    def row_copy(down, right, device):
        at = SIDES.index((down, 0))
        half = half_of(right)
        return transfer(
            sums[at].at[:, :, half],
            landed[at].at[:, :, half],
            sends,
            receives,
            half_slot(down, right),
            device,
        )

    for down, right in CORNERS:

        @pl.when(inside(row + down, col + right))
        def _():
            corner_copy(down, right, (row, col + right)).start()

    for right in (-1, 1):

        @pl.when(inside(row, col + right))
        def _():
            col_copy(right, (row, col + right)).start()

    for at, (down, right) in enumerate(SIDES[:4]):

        @pl.when(jnp.logical_not(inside(row - down, col - right)))
        def _():
            landed[at][...] = jnp.zeros(landed[at].shape, jnp.float32)

    for at in range(2):
        sums[at][...] = pieces[at][...]
    def send_half(side):
        half = half_of(side)
        for down in (-1, 1):

            @pl.when(inside(row + down, col) & inside(row, col + side))
            def _():
                corner_copy(down, -side, (row, col + side)).wait_recv()
                landing = landed[SIDES.index((down, -side))]
                sums[SIDES.index((down, 0))][:, :, half] += landing[...]

        total[:, :, half] = center[:, :, half]
        for down in (-1, 1):

            @pl.when(inside(row + down, col))
            def _():
                row_copy(down, side, (row + down, col)).start()

    @pl.when(col % 2 == 1)
    def _():
        send_half(-1)
        send_half(1)

    @pl.when(col % 2 == 0)
    def _():
        send_half(1)
        send_half(-1)

    for right in (-1, 1):

        @pl.when(inside(row, col - right))
        def _():
            col_copy(right, (row, col - right)).wait_recv()

        total[:, :, edge(-right, TILE)] += landed[SIDES.index((0, right))][...]

    for down, right in CORNERS:

        @pl.when(inside(row - down, col))
        def _():
            row_copy(down, right, (row - down, col)).wait_recv()

    for down in (-1, 1):
        total[:, edge(-down, TILE), :] += landed[SIDES.index((down, 0))][...]

    for down, right in CORNERS:

        @pl.when(inside(row + down, col + right))
        def _():
            corner_copy(down, right, (row, col + right)).wait_send()

        @pl.when(inside(row + down, col))
        def _():
            row_copy(down, right, (row + down, col)).wait_send()

    for right in (-1, 1):

        @pl.when(inside(row, col + right))
        def _():
            col_copy(right, (row, col + right)).wait_send()

    if first:
        scale = step_size / (total[2] + regular_term)
        refs[1][...] = scale
    else:
        scale = scale_in[...]
    for p in range(2):
        new[p] = own[p] - total[p] * scale


def vmem(count):
    return [pl.BlockSpec(memory_space=pltpu.VMEM)] * count


def dma_sems():
    return [pltpu.SemaphoreType.DMA((10,))] * 2


def f32(shape):
    return jax.ShapeDtypeStruct(shape, jnp.float32)


def per_device(object_field, probe_field, amplitudes, offsets, counts):
    table = jnp.asarray(dft_tables())
    offs = offsets.reshape(MAXPOS, 2).T
    cnt = counts.reshape(1)
    amps = amplitudes.reshape(MAXPOS, TILE, TILE)
    field = object_field
    edge_shapes = [f32(shape_of(2, side)) for side in SIDES]
    scale = None
    for iteration in range(ITERS):
        first = iteration == 0
        planes = 3 if first else 2
        halos = pl.pallas_call(
            halo_kernel,
            out_shape=edge_shapes,
            in_specs=vmem(1),
            out_specs=vmem(8),
            scratch_shapes=dma_sems(),
            compiler_params=pltpu.CompilerParams(collective_id=0, has_side_effects=True, vmem_limit_bytes=VMEM_LIMIT),
            cost_estimate=WIRE_COST,
            name="halo",
        )(field)
        center, *pieces = pl.pallas_call(
            functools.partial(gradient_kernel, planes),
            out_shape=[f32((planes, TILE, TILE))] + [f32(shape_of(planes, s)) for s in SIDES],
            in_specs=[pl.BlockSpec(memory_space=pltpu.SMEM)] * 2 + vmem(12),
            out_specs=vmem(9),
            scratch_shapes=[
                pltpu.VMEM((2, 5, 2 * TILE, LANES), jnp.float32),
                pltpu.VMEM((planes, 5, 2 * TILE, LANES), jnp.float32),
                pltpu.VMEM((2 * TILE, 2 * TILE), jnp.bfloat16),
                pltpu.VMEM((2 * TILE, 2 * TILE), jnp.bfloat16),
                pltpu.VMEM((2 * TILE, TILE), jnp.bfloat16),
                pltpu.VMEM((TILE, 2 * TILE), jnp.bfloat16),
                pltpu.VMEM((TILE, 2 * TILE), jnp.float32),
            ],
            compiler_params=pltpu.CompilerParams(vmem_limit_bytes=VMEM_LIMIT),
            name=f"gradient{iteration}",
        )(offs, cnt, field, *halos, probe_field, amps, table)
        operands = [field, center, *pieces] + ([] if first else [scale])
        shapes = [f32((2, TILE, TILE))]
        if first:
            shapes.append(f32((TILE, TILE)))
        results = pl.pallas_call(
            functools.partial(update_kernel, first),
            out_shape=shapes,
            in_specs=vmem(len(operands)),
            out_specs=vmem(len(shapes)),
            scratch_shapes=[pltpu.VMEM(shape_of(planes, s), jnp.float32) for s in SIDES]
            + [pltpu.VMEM((planes, RIM, TILE), jnp.float32)] * 2
            + [pltpu.VMEM((planes, TILE, TILE), jnp.float32)]
            + dma_sems(),
            compiler_params=pltpu.CompilerParams(
                collective_id=1 + iteration,
                has_side_effects=True,
                vmem_limit_bytes=VMEM_LIMIT,
            ),
            cost_estimate=WIRE_COST,
            name=f"update{iteration}",
        )(*operands)
        field = results[0]
        if first:
            scale = results[1]
    return field


def solution(mesh):
    in_specs = (
        P(None, "row", "col"),
        P(),
        P("row", "col", None, None, None),
        P("row", "col", None, None),
        P("row", "col"),
    )
    out_specs = P(None, "row", "col")
    return jax.shard_map(
        per_device, mesh=mesh, in_specs=in_specs, out_specs=out_specs, check_vma=False
    )
```
